32 devices in a mesh: row: 8 (over y, x, core), col: 4 (over z).
Axes of the slice: x: 2, y: 2, z: 4, core: 2. Of those that a mesh axis runs over, the one named last changes fastest.
Arguments:
- design_rows: bfloat16 [768, 3072], P('col', 'row'), may hold values from -1.1953125 to 1.1953125
- design_cols: bfloat16 [768, 4096], P('row', 'col'), may hold values from -1.1953125 to 1.1953125
- whitening: bfloat16 [768, 768], replicated, may hold values from -16 to 16, as said below
- epoch_mask: int32 [128], replicated, may hold values 0 or 1
- normal_old: float32 [3072, 4096], P('row', 'col'), may hold values from -6 to 6
- probes: float32 [4096, 64], P('col'), may hold values from -0.09375 to 0.09375
Outputs:
- normal_new: float32 [3072, 4096], P('row', 'col')
- products: float32 [3072, 64], P(('row', 'col'))
The draws below stay inside these ranges and needn't reach their ends.
Inputs may be any that keep to these rules, and one draw needn't show every extreme that they name: `whitening`: lower triangular with a positive diagonal.
All inputs are finite; a program needn't handle non-finite values.
Results may differ from the reference program's by a relative error of at most 0.0028.
Values may be sent and summed in bfloat16 or wider, within the bound.
No kernel may reach another device: no remote copies, remote signals or barrier semaphores. Data moves between devices by JAX's collectives and lax.ppermute only.
A program may use at most 64 MiB of HBM per device.

```python
import jax
import jax.numpy as jnp
from jax import lax

EPOCHS = 128
COMP = 6
M = 768
PROBES = 64
NR = 3072
NC = 4096


def draw_whitening(key, part):
    count = EPOCHS * COMP
    first = jax.random.fold_in(key, 11)
    second = jax.random.fold_in(key, 12)
    lower = jnp.clip(jax.random.normal(first, (count, count), jnp.float32), -4.0, 4.0)
    lower = jnp.tril(lower, -1) * (0.6 / jnp.sqrt(jnp.float32(count)))
    diag_part = 1.0 + jax.random.uniform(second, (count,), jnp.float32)
    matrix = lower + jnp.diag(diag_part)
    return matrix.astype(jnp.bfloat16)


def plant(values, rng, least, top_value):
    shape = values.shape
    place = [jax.random.randint(jax.random.fold_in(rng, axis), (), 0, shape[axis]) for axis in range(len(shape))]
    values = values.at[tuple(place)].set(least)
    longest = shape.index(max(shape))
    place[longest] = (place[longest] + 1) % shape[longest]
    return values.at[tuple(place)].set(top_value)


def shard_levels(key, dims, shards, least, top_value):
    factor_of = 1.0
    for axis_at, parts in shards:
        steps = jax.random.uniform(jax.random.fold_in(jax.random.fold_in(key, 6), axis_at), (parts,), jnp.float32, least / len(shards), top_value / len(shards))
        factor_of = factor_of * jnp.repeat(jnp.exp(steps), dims[axis_at] // parts).reshape((-1,) + (1,) * (len(dims) - 1 - axis_at))
    return factor_of


def normal_values(key, shape, deviation, reach, cuts=(), held_as=jnp.bfloat16):
    array = deviation * jax.random.normal(key, shape, jnp.float32)
    if cuts:
        array = array * shard_levels(key, shape, cuts, -0.22, 0.18)
    return jnp.clip(array, -reach, reach).astype(held_as)


def setup_inputs(seed: int = 0) -> dict:
    key_of = jax.random.split(jax.random.key(seed), 7)
    return {
        "design_rows": normal_values(key_of[0], (M, NR), 0.2, 1.1953125, ((0, 4), (1, 8))),
        "design_cols": normal_values(key_of[1], (M, NC), 0.2, 1.1953125, ((0, 8), (1, 4))),
        "whitening": draw_whitening(jax.random.fold_in(key_of[6], 71), 0),
        "epoch_mask": plant((jax.random.randint(key_of[3], (EPOCHS,), 0, 4) < 3).astype(jnp.int32), jax.random.fold_in(key_of[3], 1), 0, 1),
        "normal_old": normal_values(key_of[4], (NR, NC), 1.0, 6.0, ((0, 8), (1, 4)), jnp.float32),
        "probes": normal_values(key_of[5], (NC, PROBES), NC ** -0.5, 0.09375, ((0, 4),), jnp.float32),
    }


def reference(design_rows, design_cols, whitening, epoch_mask, normal_old, probes):
    white_rows = jnp.dot(whitening, design_rows, preferred_element_type=jnp.float32).astype(jnp.bfloat16)
    white_cols = jnp.dot(whitening, design_cols, preferred_element_type=jnp.float32)
    obs_mask = jnp.repeat(epoch_mask, COMP).astype(jnp.bfloat16)
    weighted = white_rows * obs_mask[:, None]
    gram = lax.dot_general(weighted.astype(jnp.float32), white_cols, (((0,), (0,)), ((), ())), precision=lax.Precision.HIGHEST, preferred_element_type=jnp.float32)
    normal_new = normal_old + gram
    products = jnp.dot(normal_new, probes, precision=lax.Precision.HIGHEST, preferred_element_type=jnp.float32)
    return normal_new, products
```

```python
import functools

import jax
import jax.numpy as jnp
from jax import lax
from jax.experimental import pallas as pl
from jax.experimental.pallas import tpu as pltpu
from jax.sharding import PartitionSpec as P


COMP = 6
BLOCK = 256
LIMIT = 24 << 20

F32, BF16 = jnp.float32, jnp.bfloat16
VMEM = pl.BlockSpec(memory_space=pltpu.VMEM)
NN = (((1,), (0,)), ((), ()))
NT = (((1,), (1,)), ((), ()))
TT = (((0,), (1,)), ((), ()))


def mm(a, b, dims):
    return lax.dot_general(a, b, dims, preferred_element_type=F32)


def halves(x):
    high = x.astype(BF16)
    return high, (x - high.astype(F32)).astype(BF16)


def direct(n):
    return n <= 8 and n & (n - 1) == 0


def swap(x, axis, k, n):
    return lax.ppermute(x, axis, [(i, i ^ k) for i in range(n)])


def fetch(pieces, moves, whole, sems, axis):
    me = lax.axis_index(axis)
    copies = []
    for i, (piece, k) in enumerate(zip(pieces, moves)):
        rows = piece.shape[0]
        start = pl.multiple_of((me ^ k) * rows, 16) if len(pieces) > 1 else 0
        copies.append(
            pltpu.make_async_copy(piece, whole.at[pl.ds(start, rows)], sems.at[i])
        )
        copies[-1].start()
    return copies


def cols_kernel(moves, *refs):
    n = len(moves)
    pieces, (w, probes_t, old, high, low, folded, old_part, cols, sems) = refs[:n], refs[n:]
    copies = fetch(pieces, moves, cols, sems, "row")
    size, _ = cols.shape
    count = probes_t.shape[0]
    p_high, p_low = halves(probes_t[...])
    p_both = jnp.concatenate([p_high, p_low], axis=0)
    o_high, o_low = halves(old[...])
    part = mm(p_both, o_high, NT)
    old_part[...] = part[:count] + part[count:] + mm(p_high, o_low, NT)
    for copy in copies:
        copy.wait()
    step = BLOCK if size % BLOCK == 0 else size
    for at in range(0, size, step):
        rows = slice(at, at + step)
        white = mm(w[rows, : at + step], cols[: at + step, :], NN)
        c_high, c_low = halves(white)
        high[rows, :] = c_high
        low[rows, :] = c_low
        part = mm(p_both, c_high, NT)
        total = part[:count] + part[count:] + mm(p_high, c_low, NT)
        f_high, f_low = halves(total)
        folded[:count, rows] = f_high
        folded[count:, rows] = f_low


def rows_kernel(moves, n_out, *refs):
    n = len(moves)
    pieces, (w, mask, folded, old_part, weighted) = refs[:n], refs[n : n + 5]
    outs, (rows_all, sems) = refs[n + 5 : n + 5 + n_out], refs[n + 5 + n_out :]
    copies = fetch(pieces, moves, rows_all, sems, "col")
    for copy in copies:
        copy.wait()
    size = rows_all.shape[0]
    count = old_part.shape[0]
    step = BLOCK if size % BLOCK == 0 else size
    for at in range(0, size, step):
        obs = slice(at, at + step)
        white = mm(rows_all[: at + step, :], w[obs, : at + step], TT)
        weighted[:, obs] = white.astype(BF16) * mask[:, obs]
    part = mm(folded[...], weighted[...], NT)
    part = old_part[...] + part[:count] + part[count:]
    if n_out == 1:
        outs[0][...] = part
        return
    me = lax.axis_index("col")
    chunk = part.shape[1] // n_out
    for k, out in enumerate(outs):
        value = part[:, :chunk]
        for j in range(1, n_out):
            value = jnp.where((me ^ k) == j, part[:, j * chunk : (j + 1) * chunk], value)
        out[...] = value


def gram_kernel(weighted, high, low, old, new):
    left = weighted[...]
    new[...] = old[...] + (mm(left, high[...], NN) + mm(left, low[...], NN))


def body(n_row, n_col, design_rows, design_cols, whitening, epoch_mask, normal_old, probes):
    size = whitening.shape[0]
    height, width = normal_old.shape
    count = probes.shape[1]
    mask = jnp.repeat(epoch_mask, COMP).astype(BF16)[None, :]
    probes_t = probes.T

    if direct(n_col):
        row_moves = [0] + [k for k in (2, 3, 1) if k < n_col] + list(range(4, n_col))
        rows = [design_rows] + [swap(design_rows, "col", k, n_col) for k in row_moves[1:]]
    else:
        row_moves = [0]
        rows = [lax.all_gather(design_rows, "col", axis=0, tiled=True)]
    if direct(n_row):
        far = range(2, n_row, 2)
        held = {0: design_cols, **{k: swap(design_cols, "row", k, n_row) for k in far}}
        held.update({k + 1: swap(held[k], "row", 1, n_row) for k in (0, *far)})
        col_moves, cols = list(held), list(held.values())
    else:
        col_moves, cols = [0], [lax.all_gather(design_cols, "row", axis=0, tiled=True)]

    shape = jax.ShapeDtypeStruct
    high, low, folded, old_part = pl.pallas_call(
        functools.partial(cols_kernel, col_moves),
        out_shape=[
            shape((size, width), BF16),
            shape((size, width), BF16),
            shape((2 * count, size), BF16),
            shape((count, height), F32),
        ],
        in_specs=[VMEM] * (len(cols) + 3),
        out_specs=[VMEM] * 4,
        scratch_shapes=[
            pltpu.VMEM((size, width), BF16),
            pltpu.SemaphoreType.DMA((len(cols),)),
        ],
        cost_estimate=pl.CostEstimate(
            flops=2 * size * size * width, bytes_accessed=8 * size * width, transcendentals=0
        ),
        compiler_params=pltpu.CompilerParams(vmem_limit_bytes=LIMIT),
        name="cols",
    )(*cols, whitening, probes_t, normal_old)

    n_out = n_col if direct(n_col) else 1
    chunk = height // n_out
    weighted, *parts = pl.pallas_call(
        functools.partial(rows_kernel, row_moves, n_out),
        out_shape=[shape((height, size), BF16)] + [shape((count, chunk), F32)] * n_out,
        in_specs=[VMEM] * (len(rows) + 4),
        out_specs=[VMEM] * (1 + n_out),
        scratch_shapes=[
            pltpu.VMEM((size, height), BF16),
            pltpu.SemaphoreType.DMA((len(rows),)),
        ],
        cost_estimate=pl.CostEstimate(
            flops=2 * size * size * height, bytes_accessed=6 * size * height, transcendentals=0
        ),
        compiler_params=pltpu.CompilerParams(vmem_limit_bytes=LIMIT),
        name="rows",
    )(*rows, whitening, mask, folded, old_part)

    if n_out == 1:
        products = lax.psum_scatter(parts[0], "col", scatter_dimension=1, tiled=True)
    else:
        products = parts[0]
        for k in range(n_col - 1, 0, -1):
            products = products + swap(parts[k], "col", k, n_col)

    tile = BLOCK if width % BLOCK == 0 else width
    normal_new = pl.pallas_call(
        gram_kernel,
        out_shape=shape((height, width), F32),
        grid=(width // tile,),
        in_specs=[
            pl.BlockSpec((height, size), lambda i: (0, 0)),
            pl.BlockSpec((size, tile), lambda i: (0, i)),
            pl.BlockSpec((size, tile), lambda i: (0, i)),
            pl.BlockSpec((height, tile), lambda i: (0, i)),
        ],
        out_specs=pl.BlockSpec((height, tile), lambda i: (0, i)),
        cost_estimate=pl.CostEstimate(
            flops=4 * size * height * width, bytes_accessed=8 * height * width, transcendentals=0
        ),
        compiler_params=pltpu.CompilerParams(vmem_limit_bytes=LIMIT),
        name="gram",
    )(weighted, high, low, normal_old)
    return normal_new, products.T


def solution(mesh):
    placed = (P("col", "row"), P("row", "col"), P(), P(), P("row", "col"), P("col", None))
    n_row, n_col = mesh.shape["row"], mesh.shape["col"]

    def run(*args):
        return body(n_row, n_col, *args)

    return jax.shard_map(
        run,
        mesh=mesh,
        in_specs=placed,
        out_specs=(P("row", "col"), P(("row", "col"), None)),
        check_vma=False,
    )
```

```python
import functools

import jax
import jax.numpy as jnp
from jax import lax
from jax.experimental import pallas as pl
from jax.experimental.pallas import tpu as pltpu
from jax.sharding import PartitionSpec as P


COMP = 6
BLOCK = 256
LIMIT = 24 << 20

F32, BF16 = jnp.float32, jnp.bfloat16
HBM = pl.BlockSpec(memory_space=pltpu.HBM)
VMEM = pl.BlockSpec(memory_space=pltpu.VMEM)
NN = (((1,), (0,)), ((), ()))
NT = (((1,), (1,)), ((), ()))
TT = (((0,), (1,)), ((), ()))
shape = jax.ShapeDtypeStruct


def mm(a, b, dims):
    return lax.dot_general(a, b, dims, preferred_element_type=F32)


def halves(x):
    high = x.astype(BF16)
    return high, (x - high.astype(F32)).astype(BF16)


def direct(n):
    return n <= 8 and n & (n - 1) == 0


def swap(x, axis, k, n):
    return lax.ppermute(x, axis, [(i, i ^ k) for i in range(n)])


def call(kernel, ins, outs, in_specs, out_specs, scratch, flops, limit=LIMIT):
    moved = sum(a.size * a.dtype.itemsize for a in (*ins, *outs))
    return pl.pallas_call(
        kernel,
        out_shape=outs,
        in_specs=in_specs,
        out_specs=out_specs,
        scratch_shapes=scratch,
        compiler_params=pltpu.CompilerParams(vmem_limit_bytes=limit),
        cost_estimate=pl.CostEstimate(
            flops=flops, bytes_accessed=moved, transcendentals=0
        ),
    )(*ins)


def assemble(pieces, moves, whole, axis):
    me = lax.axis_index(axis)
    for piece, k in zip(pieces, moves):
        rows = piece.shape[0]
        start = pl.multiple_of((me ^ k) * rows, 16) if len(pieces) > 1 else 0
        whole[pl.ds(start, rows), :] = piece[...]


def steps(size):
    step = BLOCK if size % BLOCK == 0 else size
    return [slice(at, at + step) for at in range(0, size, step)]


def early_kernel(old, probes_t, used, old_part, mask, old_held, probes_held, sems):
    copies = [
        pltpu.make_async_copy(probes_t, probes_held, sems.at[0]),
        pltpu.make_async_copy(old, old_held, sems.at[1]),
    ]
    for copy in copies:
        copy.start()
    count = probes_t.shape[0]
    copies[0].wait()
    p_high, p_low = halves(probes_held[...])
    both = jnp.concatenate([p_high, p_low], axis=0)
    epochs, size = used.shape[1], mask.shape[1]
    first = COMP * lax.broadcasted_iota(jnp.int32, (epochs, size), 0)
    at = lax.broadcasted_iota(jnp.int32, (epochs, size), 1)
    spread = jnp.where((at >= first) & (at < first + COMP), 1.0, 0.0).astype(BF16)
    kept = jnp.broadcast_to(used[...].astype(F32), (16, epochs)).astype(BF16)
    mask[...] = mm(kept, spread, NN)[:1].astype(BF16)
    copies[1].wait()
    o_high, o_low = halves(old_held[...])
    part = mm(both, o_high, NT)
    old_part[...] = part[:count] + part[count:] + mm(p_high, o_low, NT)


def cols_kernel(moves, *refs):
    n = len(moves)
    pieces, (w, probes_t, high, low, folded, cols, probed) = refs[:n], refs[n:]
    assemble(pieces, moves, cols, "row")
    count = probes_t.shape[0]
    p_both = jnp.concatenate(halves(probes_t[...]), axis=0)
    for obs in steps(w.shape[0]):
        both = mm(cols[obs, :], p_both, NT)
        c_high, c_low = halves(both[:, :count] + both[:, count:])
        probed[obs, :count] = c_high
        probed[obs, count:] = c_low
        seen = slice(0, obs.stop)
        c_high, c_low = halves(mm(w[obs, seen], cols[seen, :], NN))
        high[obs, :] = c_high
        low[obs, :] = c_low
        both = mm(w[obs, seen], probed[seen, :], NN)
        c_high, c_low = halves(both[:, :count] + both[:, count:])
        folded[obs, :count] = c_high
        folded[obs, count:] = c_low


def rows_kernel(moves, n_out, *refs):
    n = len(moves)
    pieces, (w, mask, folded, old_part, weighted) = refs[:n], refs[n : n + 5]
    outs, (rows,) = refs[n + 5 : n + 5 + n_out], refs[n + 5 + n_out :]
    assemble(pieces, moves, rows, "col")
    count = old_part.shape[0]
    for obs in steps(w.shape[0]):
        seen = slice(0, obs.stop)
        white = mm(rows[seen, :], w[obs, seen], TT)
        weighted[:, obs] = white.astype(BF16) * mask[:, obs]
    both = mm(weighted[...], folded[...], NN)
    part = old_part[...] + (both[:, :count] + both[:, count:]).T
    if n_out == 1:
        outs[0][...] = part
        return
    me = lax.axis_index("col")
    chunk = part.shape[1] // n_out
    for k, out in enumerate(outs):
        value = part[:, :chunk]
        for j in range(1, n_out):
            value = jnp.where((me ^ k) == j, part[:, j * chunk : (j + 1) * chunk], value)
        out[...] = value


def gram_kernel(weighted, high, low, old, new, made, sems):
    left = weighted[...]
    copies = []
    for i, at in enumerate(steps(old.shape[1])):
        made[:, at] = old[:, at] + (mm(left, high[:, at], NN) + mm(left, low[:, at], NN))
        copies.append(pltpu.make_async_copy(made.at[:, at], new.at[:, at], sems.at[i]))
        copies[-1].start()
    for copy in copies:
        copy.wait()


def body(n_row, n_col, design_rows, design_cols, whitening, epoch_mask, normal_old, probes):
    size = whitening.shape[0]
    height, width = normal_old.shape
    count = probes.shape[1]
    fast = direct(n_col) and direct(n_row)

    old_part, mask = call(
        early_kernel,
        (normal_old, probes.T, epoch_mask[None, :]),
        [shape((count, height), F32), shape((1, size), BF16)],
        [HBM] * 2 + [VMEM],
        [VMEM] * 2,
        [
            pltpu.VMEM((height, width), F32),
            pltpu.VMEM((count, width), F32),
            pltpu.SemaphoreType.DMA((2,)),
        ],
        64 * count * height * width,
        58 << 20,
    )

    if fast:
        row_moves = list(range(n_col))
        rows = [design_rows] + [swap(design_rows, "col", k, n_col) for k in row_moves[1:]]
        far = range(2, n_row, 2)
        held = {0: design_cols, **{k: swap(design_cols, "row", k, n_row) for k in far}}
        held.update({k + 1: swap(held[k], "row", 1, n_row) for k in (0, *far)})
        col_moves, cols = list(held), list(held.values())
    else:
        row_moves = col_moves = [0]
        rows = [lax.all_gather(design_rows, "col", axis=0, tiled=True)]
        cols = [lax.all_gather(design_cols, "row", axis=0, tiled=True)]

    high, low, folded = call(
        functools.partial(cols_kernel, col_moves),
        (*cols, whitening, probes.T),
        [shape((size, width), BF16)] * 2 + [shape((size, 2 * count), BF16)],
        [VMEM] * (len(cols) + 2),
        [VMEM] * 3,
        [pltpu.VMEM((size, width), BF16), pltpu.VMEM((size, 2 * count), BF16)],
        2 * size * size * width,
    )
    n_out = n_col if fast else 1
    weighted, *parts = call(
        functools.partial(rows_kernel, row_moves, n_out),
        (*rows, whitening, mask, folded, old_part),
        [shape((height, size), BF16)] + [shape((count, height // n_out), F32)] * n_out,
        [VMEM] * (len(rows) + 4),
        [VMEM] * (1 + n_out),
        [pltpu.VMEM((size, height), BF16)],
        2 * size * size * height,
    )
    if fast:
        products = parts[0]
        for k in range(n_col - 1, 0, -1):
            products = products + swap(parts[k], "col", k, n_col)
    else:
        products = lax.psum_scatter(parts[0], "col", scatter_dimension=1, tiled=True)
    normal_new = call(
        gram_kernel,
        (weighted, high, low, normal_old),
        [shape((height, width), F32)],
        [VMEM] * 4,
        [HBM],
        [pltpu.VMEM((height, width), F32), pltpu.SemaphoreType.DMA((len(steps(width)),))],
        4 * size * height * width,
    )[0]
    return normal_new, products.T


def solution(mesh):
    placed = (P("col", "row"), P("row", "col"), P(), P(), P("row", "col"), P("col", None))
    n_row, n_col = mesh.shape["row"], mesh.shape["col"]

    def run(*args):
        return body(n_row, n_col, *args)

    return jax.shard_map(
        run,
        mesh=mesh,
        in_specs=placed,
        out_specs=(P("row", "col"), P(("row", "col"), None)),
        check_vma=False,
    )
```

```python
import functools

import jax
import jax.numpy as jnp
from jax import lax
from jax.experimental import pallas as pl
from jax.experimental.pallas import tpu as pltpu
from jax.sharding import PartitionSpec as P


COMP = 6
BLOCK = 256
LIMIT = 24 << 20

F32, BF16 = jnp.float32, jnp.bfloat16
HBM = pl.BlockSpec(memory_space=pltpu.HBM)
VMEM = pl.BlockSpec(memory_space=pltpu.VMEM)
NN = (((1,), (0,)), ((), ()))
NT = (((1,), (1,)), ((), ()))
TT = (((0,), (1,)), ((), ()))
shape = jax.ShapeDtypeStruct


def mm(a, b, dims):
    return lax.dot_general(a, b, dims, preferred_element_type=F32)


def halves(x):
    high = x.astype(BF16)
    return high, (x - high.astype(F32)).astype(BF16)


def halves_sum(x, axis=1):
    first, second = jnp.split(x, 2, axis=axis)
    return first + second


def swap(x, axis, k, n):
    return lax.ppermute(x, axis, [(i, i ^ k) for i in range(n)])


def tick_kernel(out):
    out[...] = jnp.zeros_like(out)


def tick(cost):
    return pl.pallas_call(
        tick_kernel,
        out_shape=shape((8, 128), F32),
        out_specs=VMEM,
        compiler_params=pltpu.CompilerParams(vmem_limit_bytes=LIMIT),
        cost_estimate=pl.CostEstimate(flops=cost, bytes_accessed=4096, transcendentals=0),
        name="tick",
    )()


def call(kernel, ins, outs, in_specs, scratch, flops, out_specs=None, limit=LIMIT):
    moved = sum(a.size * a.dtype.itemsize for a in (*ins, *outs))
    return pl.pallas_call(
        kernel,
        out_shape=outs,
        in_specs=in_specs,
        out_specs=out_specs or [VMEM] * len(outs),
        scratch_shapes=scratch,
        compiler_params=pltpu.CompilerParams(vmem_limit_bytes=limit),
        cost_estimate=pl.CostEstimate(
            flops=flops, bytes_accessed=moved, transcendentals=0
        ),
    )(*ins)


def steps(size):
    step = BLOCK if size % BLOCK == 0 else size
    return [slice(at, at + step) for at in range(0, size, step)]


def beside(a, b):
    return jnp.concatenate([a, b], axis=1)


def early_kernel(old, probes_t, used, marker, old_part, both, mask):
    p_high, p_low = halves(probes_t[...])
    both[...] = jnp.concatenate([p_high, p_low], axis=0)
    o_high, o_low = halves(old[...])
    old_part[...] = mm(o_high, both[...], NT) + mm(o_low, both[...], NT)
    epochs, size = used.shape[1], mask.shape[1]
    first = COMP * lax.broadcasted_iota(jnp.int32, (epochs, size), 0)
    at = lax.broadcasted_iota(jnp.int32, (epochs, size), 1)
    spread = jnp.where((at >= first) & (at < first + COMP), 1.0, 0.0).astype(BF16)
    kept = jnp.broadcast_to(used[...].astype(F32), (16, epochs)).astype(BF16)
    mask[...] = mm(kept, spread, NN)[:1].astype(BF16)


def place(whole, axis, k, value):
    start = pl.multiple_of((lax.axis_index(axis) ^ k) * value.shape[0], 16)
    whole[pl.ds(start, value.shape[0]), :] = value


def probe(pieces, both, probed, moves):
    rows = jnp.concatenate([piece[...] for piece in pieces], axis=0)
    found = beside(*halves(mm(rows, both[...], NT)))
    count = pieces[0].shape[0]
    for i, k in enumerate(moves):
        place(probed, "row", k, found[i * count : (i + 1) * count])


def near_kernel(moves, *refs):
    pieces, (both, known) = refs[: len(moves)], refs[len(moves) :]
    known[...] = jnp.zeros_like(known)
    probe(pieces, both, known, moves)


def cols_kernel(moves, *refs):
    pieces, (both, known, w, folded, probed) = refs[: len(moves)], refs[len(moves) :]
    probed[...] = known[...]
    probe(pieces, both, probed, moves)
    for obs in steps(w.shape[0]):
        seen = slice(0, obs.stop)
        folded[obs, :] = beside(*halves(halves_sum(mm(w[obs, seen], probed[seen, :], NN))))


def rows_kernel(moves, *refs):
    n = len(moves)
    pieces, (folded, w, mask, old_part, weighted) = refs[:n], refs[n : n + 5]
    outs, (rows, part) = refs[n + 5 : 2 * n + 5], refs[2 * n + 5 :]
    for piece, k in zip(pieces, moves):
        place(rows, "col", k, piece[...])
    for obs in steps(w.shape[0]):
        seen = slice(0, obs.stop)
        white = mm(rows[seen, :], w[obs, seen], TT)
        weighted[:, obs] = white.astype(BF16) * mask[:, obs]
    part[...] = old_part[...] + halves_sum(mm(weighted[...], folded[...], NN))
    me = lax.axis_index("col")
    chunk = part.shape[0] // n
    for k, out in enumerate(outs):
        mine = part[pl.ds(pl.multiple_of((me ^ k) * chunk, 8), chunk), :]
        out[...] = halves_sum(mine.T, axis=0)


def gram_kernel(moves, *refs):
    n = len(moves)
    pieces, (w, weighted, old, new, cols, high, low, made, sems) = refs[:n], refs[n:]
    for piece, k in zip(pieces, moves):
        place(cols, "row", k, piece[...])
    left = weighted[...]
    copies = []
    for i, at in enumerate(steps(old.shape[1])):
        for obs in steps(w.shape[0]):
            seen = slice(0, obs.stop)
            c_high, c_low = halves(mm(w[obs, seen], cols[seen, at], NN))
            high[obs, at] = c_high
            low[obs, at] = c_low
        made[:, at] = old[:, at] + (mm(left, high[:, at], NN) + mm(left, low[:, at], NN))
        copies.append(pltpu.make_async_copy(made.at[:, at], new.at[:, at], sems.at[i]))
        copies[-1].start()
    for copy in copies:
        copy.wait()


def tuned(n_row, n_col):
    return n_col == 4 and n_row in (4, 8)


def body(n_row, n_col, design_rows, design_cols, whitening, epoch_mask, normal_old, probes):
    size = whitening.shape[0]
    height, width = normal_old.shape
    count = probes.shape[1]
    far = range(2, n_row, 2)

    row_moves = list(range(n_col))
    rows = [design_rows] + [swap(design_rows, "col", k, n_col) for k in row_moves[1:]]
    marker = tick(64 * size * height * width)
    held = {0: design_cols, **{k: swap(design_cols, "row", k, n_row) for k in far}}
    held.update({k + 1: swap(held[k], "row", 1, n_row) for k in (0, *far)})

    old_part, both, mask = call(
        early_kernel,
        (normal_old, probes.T, epoch_mask[None, :], marker),
        [
            shape((height, 2 * count), F32),
            shape((2 * count, width), BF16),
            shape((1, size), BF16),
        ],
        [VMEM] * 4,
        [],
        6 * count * height * width,
    )
    last = [k for k in held if k in LAST]
    soon = [k for k in held if k not in LAST]
    known = call(
        functools.partial(near_kernel, soon),
        (*(held[k] for k in soon), both),
        [shape((size, 4 * count), BF16)],
        [VMEM] * (len(soon) + 1),
        [],
        4 * size * width * count,
    )[0]
    folded = call(
        functools.partial(cols_kernel, last),
        (*(held[k] for k in last), both, known, whitening),
        [shape((size, 4 * count), BF16)],
        [VMEM] * (len(last) + 3),
        [pltpu.VMEM((size, 4 * count), BF16)],
        4 * size * size * count,
    )[0]
    weighted, *parts = call(
        functools.partial(rows_kernel, row_moves),
        (*rows, folded, whitening, mask, old_part),
        [shape((height, size), BF16)] + [shape((count, height // n_col), F32)] * n_col,
        [VMEM] * (len(rows) + 4),
        [pltpu.VMEM((size, height), BF16), pltpu.VMEM((height, 2 * count), F32)],
        2 * size * size * height,
    )
    products = parts[0]
    for k in range(n_col - 1, 0, -1):
        products = products + swap(parts[k], "col", k, n_col)
    normal_new = call(
        functools.partial(gram_kernel, list(held)),
        (*held.values(), whitening, weighted, normal_old),
        [shape((height, width), F32)],
        [VMEM] * (len(held) + 3),
        [pltpu.VMEM((size, width), BF16)] * 3
        + [pltpu.VMEM((height, width), F32), pltpu.SemaphoreType.DMA((len(steps(width)),))],
        4 * size * height * width,
        out_specs=[HBM],
    )[0]
    return normal_new, products.T


def plain(design_rows, design_cols, whitening, epoch_mask, normal_old, probes):
    high = lax.Precision.HIGHEST
    mask = jnp.repeat(epoch_mask, COMP).astype(BF16)
    rows = lax.all_gather(design_rows, "col", axis=0, tiled=True)
    cols = lax.all_gather(design_cols, "row", axis=0, tiled=True)
    weighted = mm(whitening, rows, NN).astype(BF16) * mask[:, None]
    white = mm(whitening, cols, NN)
    gram = jnp.dot(weighted.astype(F32).T, white, precision=high)
    normal_new = normal_old + gram
    part = jnp.dot(normal_new, probes, precision=high)
    return normal_new, lax.psum_scatter(part, "col", scatter_dimension=0, tiled=True)


LAST = (3, 5, 7)


def solution(mesh):
    placed = (P("col", "row"), P("row", "col"), P(), P(), P("row", "col"), P("col", None))
    n_row, n_col = mesh.shape["row"], mesh.shape["col"]
    fast = tuned(n_row, n_col)

    def run(*args):
        return body(n_row, n_col, *args) if fast else plain(*args)

    return jax.shard_map(
        run,
        mesh=mesh,
        in_specs=placed,
        out_specs=(P("row", "col"), P(("row", "col"), None)),
        check_vma=False,
    )
```

```python
import functools

import jax
import jax.numpy as jnp
from jax import lax
from jax.experimental import pallas as pl
from jax.experimental.pallas import tpu as pltpu
from jax.sharding import PartitionSpec as P


COMP = 6
BLOCK = 256
LIMIT = 24 << 20

F32, BF16 = jnp.float32, jnp.bfloat16
HBM = pl.BlockSpec(memory_space=pltpu.HBM)
VMEM = pl.BlockSpec(memory_space=pltpu.VMEM)
NN = (((1,), (0,)), ((), ()))
NT = (((1,), (1,)), ((), ()))
TT = (((0,), (1,)), ((), ()))
shape = jax.ShapeDtypeStruct


def mm(a, b, dims):
    return lax.dot_general(a, b, dims, preferred_element_type=F32)


def halves(x):
    high = x.astype(BF16)
    return high, (x - high.astype(F32)).astype(BF16)


def halves_sum(x, axis=1):
    first, second = jnp.split(x, 2, axis=axis)
    return first + second


def swap(x, axis, k, n):
    return lax.ppermute(x, axis, [(i, i ^ k) for i in range(n)])


def fold(i):
    return i ^ (i >> 1)


def ahead(i, k, n):
    return fold((fold(i) + k) % n)


def turn(x, axis, k, n):
    return lax.ppermute(x, axis, [(i, ahead(i, k, n)) for i in range(n)])


def tick_kernel(out):
    out[...] = jnp.zeros_like(out)


def tick(cost):
    return pl.pallas_call(
        tick_kernel,
        out_shape=shape((8, 128), F32),
        out_specs=VMEM,
        compiler_params=pltpu.CompilerParams(vmem_limit_bytes=LIMIT),
        cost_estimate=pl.CostEstimate(flops=cost, bytes_accessed=4096, transcendentals=0),
        name="tick",
    )()


def call(kernel, ins, outs, in_specs, scratch, flops, out_specs=None, limit=LIMIT):
    moved = sum(a.size * a.dtype.itemsize for a in (*ins, *outs))
    return pl.pallas_call(
        kernel,
        out_shape=outs,
        in_specs=in_specs,
        out_specs=out_specs or [VMEM] * len(outs),
        scratch_shapes=scratch,
        compiler_params=pltpu.CompilerParams(vmem_limit_bytes=limit),
        cost_estimate=pl.CostEstimate(
            flops=flops, bytes_accessed=moved, transcendentals=0
        ),
    )(*ins)


def steps(size):
    step = BLOCK if size % BLOCK == 0 else size
    return [slice(at, at + step) for at in range(0, size, step)]


def beside(a, b):
    return jnp.concatenate([a, b], axis=1)


def early_kernel(old, probes_t, used, marker, old_part, both, mask):
    p_high, p_low = halves(probes_t[...])
    both[...] = jnp.concatenate([p_high, p_low], axis=0)
    o_high, o_low = halves(old[...])
    old_part[...] = mm(o_high, both[...], NT) + mm(o_low, both[...], NT)
    epochs, size = used.shape[1], mask.shape[1]
    first = COMP * lax.broadcasted_iota(jnp.int32, (epochs, size), 0)
    at = lax.broadcasted_iota(jnp.int32, (epochs, size), 1)
    spread = jnp.where((at >= first) & (at < first + COMP), 1.0, 0.0).astype(BF16)
    kept = jnp.broadcast_to(used[...].astype(F32), (16, epochs)).astype(BF16)
    mask[...] = mm(kept, spread, NN)[:1].astype(BF16)


def place(whole, axis, k, value):
    start = pl.multiple_of((lax.axis_index(axis) ^ k) * value.shape[0], 16)
    whole[pl.ds(start, value.shape[0]), :] = value


def probe(pieces, both, probed, moves):
    rows = jnp.concatenate([piece[...] for piece in pieces], axis=0)
    found = beside(*halves(mm(rows, both[...], NT)))
    count = pieces[0].shape[0]
    for i, k in enumerate(moves):
        place(probed, "row", k, found[i * count : (i + 1) * count])


def near_kernel(moves, *refs):
    pieces, (both, known) = refs[: len(moves)], refs[len(moves) :]
    known[...] = jnp.zeros_like(known)
    probe(pieces, both, known, moves)


def cols_kernel(moves, *refs):
    pieces, (both, known, w, folded, probed) = refs[: len(moves)], refs[len(moves) :]
    probed[...] = known[...]
    probe(pieces, both, probed, moves)
    for obs in steps(w.shape[0]):
        seen = slice(0, obs.stop)
        folded[obs, :] = beside(*halves(halves_sum(mm(w[obs, seen], probed[seen, :], NN))))


def rows_kernel(moves, *refs):
    n = len(moves)
    pieces, (folded, w, mask, old_part, weighted) = refs[:n], refs[n : n + 5]
    outs, (rows, part) = refs[n + 5 : 2 * n + 5], refs[2 * n + 5 :]
    me = lax.axis_index("col")
    for piece, k in zip(pieces, moves):
        count = piece.shape[0]
        rows[pl.ds(pl.multiple_of((me ^ k) * count, 16), count), :] = piece[...]
    for obs in steps(w.shape[0]):
        seen = slice(0, obs.stop)
        white = mm(rows[seen, :], w[obs, seen], TT)
        weighted[:, obs] = white.astype(BF16) * mask[:, obs]
    part[...] = old_part[...] + halves_sum(mm(weighted[...], folded[...], NN))
    chunk = part.shape[0] // n
    for k, out in enumerate(outs):
        mine = part[pl.ds(pl.multiple_of(ahead(me, k, n) * chunk, 8), chunk), :]
        out[...] = halves_sum(mine.T, axis=0)


def gram_kernel(moves, *refs):
    n = len(moves)
    pieces, (w, weighted, old, new, cols, high, low, made, sems) = refs[:n], refs[n:]
    for piece, k in zip(pieces, moves):
        place(cols, "row", k, piece[...])
    left = weighted[...]
    copies = []
    for i, at in enumerate(steps(old.shape[1])):
        for obs in steps(w.shape[0]):
            seen = slice(0, obs.stop)
            c_high, c_low = halves(mm(w[obs, seen], cols[seen, at], NN))
            high[obs, at] = c_high
            low[obs, at] = c_low
        made[:, at] = old[:, at] + (mm(left, high[:, at], NN) + mm(left, low[:, at], NN))
        copies.append(pltpu.make_async_copy(made.at[:, at], new.at[:, at], sems.at[i]))
        copies[-1].start()
    for copy in copies:
        copy.wait()


def tuned(n_row, n_col):
    return n_col == 4 and n_row in (4, 8)


def body(n_row, n_col, design_rows, design_cols, whitening, epoch_mask, normal_old, probes):
    size = whitening.shape[0]
    height, width = normal_old.shape
    count = probes.shape[1]
    far = range(2, n_row, 2)

    row_moves = list(range(n_col))
    rows = [design_rows] + [swap(design_rows, "col", k, n_col) for k in row_moves[1:]]
    marker = tick(64 * size * height * width)
    held = {0: design_cols, **{k: swap(design_cols, "row", k, n_row) for k in far}}
    held.update({k + 1: swap(held[k], "row", 1, n_row) for k in (0, *far)})

    old_part, both, mask = call(
        early_kernel,
        (normal_old, probes.T, epoch_mask[None, :], marker),
        [
            shape((height, 2 * count), F32),
            shape((2 * count, width), BF16),
            shape((1, size), BF16),
        ],
        [VMEM] * 4,
        [],
        6 * count * height * width,
    )
    last = [k for k in held if k in LAST]
    soon = [k for k in held if k not in LAST]
    known = call(
        functools.partial(near_kernel, soon),
        (*(held[k] for k in soon), both),
        [shape((size, 4 * count), BF16)],
        [VMEM] * (len(soon) + 1),
        [],
        4 * size * width * count,
    )[0]
    folded = call(
        functools.partial(cols_kernel, last),
        (*(held[k] for k in last), both, known, whitening),
        [shape((size, 4 * count), BF16)],
        [VMEM] * (len(last) + 3),
        [pltpu.VMEM((size, 4 * count), BF16)],
        4 * size * size * count,
    )[0]
    weighted, *parts = call(
        functools.partial(rows_kernel, row_moves),
        (*rows, folded, whitening, mask, old_part),
        [shape((height, size), BF16)] + [shape((count, height // n_col), F32)] * n_col,
        [VMEM] * (len(rows) + 4),
        [pltpu.VMEM((size, height), BF16), pltpu.VMEM((height, 2 * count), F32)],
        2 * size * size * height,
    )
    products = parts[0]
    for k in range(n_col - 1, 0, -1):
        products = products + turn(parts[k], "col", k, n_col)
    normal_new = call(
        functools.partial(gram_kernel, list(held)),
        (*held.values(), whitening, weighted, normal_old),
        [shape((height, width), F32)],
        [VMEM] * (len(held) + 3),
        [pltpu.VMEM((size, width), BF16)] * 3
        + [pltpu.VMEM((height, width), F32), pltpu.SemaphoreType.DMA((len(steps(width)),))],
        4 * size * height * width,
        out_specs=[HBM],
    )[0]
    return normal_new, products.T


def plain(design_rows, design_cols, whitening, epoch_mask, normal_old, probes):
    high = lax.Precision.HIGHEST
    mask = jnp.repeat(epoch_mask, COMP).astype(BF16)
    rows = lax.all_gather(design_rows, "col", axis=0, tiled=True)
    cols = lax.all_gather(design_cols, "row", axis=0, tiled=True)
    weighted = mm(whitening, rows, NN).astype(BF16) * mask[:, None]
    white = mm(whitening, cols, NN)
    gram = jnp.dot(weighted.astype(F32).T, white, precision=high)
    normal_new = normal_old + gram
    part = jnp.dot(normal_new, probes, precision=high)
    return normal_new, lax.psum_scatter(part, "col", scatter_dimension=0, tiled=True)


LAST = (3, 5, 7)


def solution(mesh):
    placed = (P("col", "row"), P("row", "col"), P(), P(), P("row", "col"), P("col", None))
    n_row, n_col = mesh.shape["row"], mesh.shape["col"]
    fast = tuned(n_row, n_col)

    def run(*args):
        return body(n_row, n_col, *args) if fast else plain(*args)

    return jax.shard_map(
        run,
        mesh=mesh,
        in_specs=placed,
        out_specs=(P("row", "col"), P(("row", "col"), None)),
        check_vma=False,
    )
```

```python
import functools

import jax
import jax.numpy as jnp
from jax import lax
from jax.experimental import pallas as pl
from jax.experimental.pallas import tpu as pltpu
from jax.sharding import PartitionSpec as P


COMP = 6
BLOCK = 256
LIMIT = 24 << 20

F32, BF16 = jnp.float32, jnp.bfloat16
HBM = pl.BlockSpec(memory_space=pltpu.HBM)
VMEM = pl.BlockSpec(memory_space=pltpu.VMEM)
NN = (((1,), (0,)), ((), ()))
NT = (((1,), (1,)), ((), ()))
TT = (((0,), (1,)), ((), ()))
shape = jax.ShapeDtypeStruct


def mm(a, b, dims):
    return lax.dot_general(a, b, dims, preferred_element_type=F32)


def halves(x):
    high = x.astype(BF16)
    return high, (x - high.astype(F32)).astype(BF16)


def halves_sum(x, axis=1):
    first, second = jnp.split(x, 2, axis=axis)
    return first + second


def swap(x, axis, k, n):
    return lax.ppermute(x, axis, [(i, i ^ k) for i in range(n)])


def fold(i):
    return i ^ (i >> 1)


def ahead(i, k, n):
    return fold((fold(i) + k) % n)


def turn(x, axis, k, n):
    return lax.ppermute(x, axis, [(i, ahead(i, k, n)) for i in range(n)])


def tick_kernel(out):
    out[...] = jnp.zeros_like(out)


def tick(cost):
    return pl.pallas_call(
        tick_kernel,
        out_shape=shape((8, 128), F32),
        out_specs=VMEM,
        compiler_params=pltpu.CompilerParams(vmem_limit_bytes=LIMIT),
        cost_estimate=pl.CostEstimate(flops=cost, bytes_accessed=4096, transcendentals=0),
        name="tick",
    )()


def call(kernel, ins, outs, in_specs, scratch, flops, out_specs=None, limit=LIMIT):
    moved = sum(a.size * a.dtype.itemsize for a in (*ins, *outs))
    return pl.pallas_call(
        kernel,
        out_shape=outs,
        in_specs=in_specs,
        out_specs=out_specs or [VMEM] * len(outs),
        scratch_shapes=scratch,
        compiler_params=pltpu.CompilerParams(vmem_limit_bytes=limit),
        cost_estimate=pl.CostEstimate(
            flops=flops, bytes_accessed=moved, transcendentals=0
        ),
    )(*ins)


def steps(size):
    step = BLOCK if size % BLOCK == 0 else size
    return [slice(at, at + step) for at in range(0, size, step)]


def beside(a, b):
    return jnp.concatenate([a, b], axis=1)


def early_kernel(old, probes_t, used, marker, old_part, both, mask):
    p_high, p_low = halves(probes_t[...])
    both[...] = jnp.concatenate([p_high, p_low], axis=0)
    o_high, o_low = halves(old[...])
    old_part[...] = mm(o_high, both[...], NT) + mm(o_low, both[...], NT)
    epochs, size = used.shape[1], mask.shape[1]
    first = COMP * lax.broadcasted_iota(jnp.int32, (epochs, size), 0)
    at = lax.broadcasted_iota(jnp.int32, (epochs, size), 1)
    spread = jnp.where((at >= first) & (at < first + COMP), 1.0, 0.0).astype(BF16)
    kept = jnp.broadcast_to(used[...].astype(F32), (16, epochs)).astype(BF16)
    mask[...] = mm(kept, spread, NN)[:1].astype(BF16)


def place(whole, axis, k, value):
    start = pl.multiple_of((lax.axis_index(axis) ^ k) * value.shape[0], 16)
    whole[pl.ds(start, value.shape[0]), :] = value


def probe(pieces, both, probed, moves):
    rows = jnp.concatenate([piece[...] for piece in pieces], axis=0)
    found = beside(*halves(mm(rows, both[...], NT)))
    count = pieces[0].shape[0]
    for i, k in enumerate(moves):
        place(probed, "row", k, found[i * count : (i + 1) * count])


def near_kernel(moves, *refs):
    pieces, (both, known) = refs[: len(moves)], refs[len(moves) :]
    known[...] = jnp.zeros_like(known)
    probe(pieces, both, known, moves)


def cols_kernel(moves, *refs):
    pieces, (both, known, w, folded, probed) = refs[: len(moves)], refs[len(moves) :]
    probed[...] = known[...]
    probe(pieces, both, probed, moves)
    for obs in steps(w.shape[0]):
        seen = slice(0, obs.stop)
        folded[obs, :] = beside(*halves(halves_sum(mm(w[obs, seen], probed[seen, :], NN))))


def rows_kernel(moves, *refs):
    n = len(moves)
    pieces, (folded, w, mask, old_part, weighted) = refs[:n], refs[n : n + 5]
    outs, (rows, part) = refs[n + 5 : 2 * n + 5], refs[2 * n + 5 :]
    me = lax.axis_index("col")
    for piece, k in zip(pieces, moves):
        count = piece.shape[0]
        start = ahead(me, n - k, n) * count
        rows[pl.ds(pl.multiple_of(start, 16), count), :] = piece[...]
    for obs in steps(w.shape[0]):
        seen = slice(0, obs.stop)
        white = mm(rows[seen, :], w[obs, seen], TT)
        weighted[:, obs] = white.astype(BF16) * mask[:, obs]
    part[...] = old_part[...] + halves_sum(mm(weighted[...], folded[...], NN))
    chunk = part.shape[0] // n
    for k, out in enumerate(outs):
        mine = part[pl.ds(pl.multiple_of(ahead(me, k, n) * chunk, 8), chunk), :]
        out[...] = halves_sum(mine.T, axis=0)


def gram_kernel(moves, *refs):
    n = len(moves)
    pieces, (w, weighted, old, new, cols, high, low, made, sems) = refs[:n], refs[n:]
    for piece, k in zip(pieces, moves):
        place(cols, "row", k, piece[...])
    left = weighted[...]
    copies = []
    for i, at in enumerate(steps(old.shape[1])):
        for obs in steps(w.shape[0]):
            seen = slice(0, obs.stop)
            c_high, c_low = halves(mm(w[obs, seen], cols[seen, at], NN))
            high[obs, at] = c_high
            low[obs, at] = c_low
        made[:, at] = old[:, at] + (mm(left, high[:, at], NN) + mm(left, low[:, at], NN))
        copies.append(pltpu.make_async_copy(made.at[:, at], new.at[:, at], sems.at[i]))
        copies[-1].start()
    for copy in copies:
        copy.wait()


def tuned(n_row, n_col):
    return n_col == 4 and n_row in (4, 8)


def body(n_row, n_col, design_rows, design_cols, whitening, epoch_mask, normal_old, probes):
    size = whitening.shape[0]
    height, width = normal_old.shape
    count = probes.shape[1]
    far = range(2, n_row, 2)

    row_moves = list(range(n_col))
    rows = [design_rows] + [turn(design_rows, "col", k, n_col) for k in row_moves[1:]]
    marker = tick(64 * size * height * width)
    held = {0: design_cols, **{k: swap(design_cols, "row", k, n_row) for k in far}}
    held.update({k + 1: swap(held[k], "row", 1, n_row) for k in (0, *far)})

    old_part, both, mask = call(
        early_kernel,
        (normal_old, probes.T, epoch_mask[None, :], marker),
        [
            shape((height, 2 * count), F32),
            shape((2 * count, width), BF16),
            shape((1, size), BF16),
        ],
        [VMEM] * 4,
        [],
        6 * count * height * width,
    )
    last = [k for k in held if k in LAST]
    soon = [k for k in held if k not in LAST]
    known = call(
        functools.partial(near_kernel, soon),
        (*(held[k] for k in soon), both),
        [shape((size, 4 * count), BF16)],
        [VMEM] * (len(soon) + 1),
        [],
        4 * size * width * count,
    )[0]
    folded = call(
        functools.partial(cols_kernel, last),
        (*(held[k] for k in last), both, known, whitening),
        [shape((size, 4 * count), BF16)],
        [VMEM] * (len(last) + 3),
        [pltpu.VMEM((size, 4 * count), BF16)],
        4 * size * size * count,
    )[0]
    weighted, *parts = call(
        functools.partial(rows_kernel, row_moves),
        (*rows, folded, whitening, mask, old_part),
        [shape((height, size), BF16)] + [shape((count, height // n_col), F32)] * n_col,
        [VMEM] * (len(rows) + 4),
        [pltpu.VMEM((size, height), BF16), pltpu.VMEM((height, 2 * count), F32)],
        2 * size * size * height,
    )
    products = parts[0]
    for k in range(n_col - 1, 0, -1):
        products = products + turn(parts[k], "col", k, n_col)
    normal_new = call(
        functools.partial(gram_kernel, list(held)),
        (*held.values(), whitening, weighted, normal_old),
        [shape((height, width), F32)],
        [VMEM] * (len(held) + 3),
        [pltpu.VMEM((size, width), BF16)] * 3
        + [pltpu.VMEM((height, width), F32), pltpu.SemaphoreType.DMA((len(steps(width)),))],
        4 * size * height * width,
        out_specs=[HBM],
    )[0]
    return normal_new, products.T


def plain(design_rows, design_cols, whitening, epoch_mask, normal_old, probes):
    high = lax.Precision.HIGHEST
    mask = jnp.repeat(epoch_mask, COMP).astype(BF16)
    rows = lax.all_gather(design_rows, "col", axis=0, tiled=True)
    cols = lax.all_gather(design_cols, "row", axis=0, tiled=True)
    weighted = mm(whitening, rows, NN).astype(BF16) * mask[:, None]
    white = mm(whitening, cols, NN)
    gram = jnp.dot(weighted.astype(F32).T, white, precision=high)
    normal_new = normal_old + gram
    part = jnp.dot(normal_new, probes, precision=high)
    return normal_new, lax.psum_scatter(part, "col", scatter_dimension=0, tiled=True)


LAST = (3, 5)


def solution(mesh):
    placed = (P("col", "row"), P("row", "col"), P(), P(), P("row", "col"), P("col", None))
    n_row, n_col = mesh.shape["row"], mesh.shape["col"]
    fast = tuned(n_row, n_col)

    def run(*args):
        return body(n_row, n_col, *args) if fast else plain(*args)

    return jax.shard_map(
        run,
        mesh=mesh,
        in_specs=placed,
        out_specs=(P("row", "col"), P(("row", "col"), None)),
        check_vma=False,
    )
```
